32 devices in a mesh: parts: 2 (over x), row: 16 (over z, y, core).
Axes of the slice: x: 2, y: 2, z: 4, core: 2. Of those that a mesh axis runs over, the one named last changes fastest.
Arguments:
- records: bfloat16 [128, 3, 1, 6144], P(('parts', 'row')), parts along dimension 0, may hold values from -120 to 120
- counts: int32 [32], P(('parts', 'row')), parts along dimension 0, may hold values from 1 to 4, 32 in all
- assign: int32 [64], P('parts'), parts along dimension 0, may hold values from 0 to 31, each once
- station_slot: int32 [64], P('parts'), parts along dimension 0, may hold values from 0 to 31, each once
- gap_mask: int32 [64, 1], P('parts'), parts along dimension 0, may hold values 0 or 1
Outputs:
- correlations: float32 [64, 32, 9, 512], P(('parts', 'row')), parts along dimension 0
The draws below stay inside these ranges and needn't reach their ends.
There are 2 independent parts, one for each index of `parts`. The reference program is written for one: setup_inputs(seed, part) draws one part's arguments, and reference() takes and returns one part's arrays. A program takes and returns all parts, laid end to end along the dimension named above; each array names one. Nothing has to cross between parts.
Inputs may be any that keep to these rules, and one draw needn't show every extreme that they name: The counts of one region sum to 32; the largest is 4. `assign`: each station once. `station_slot`: each row once.
All inputs are finite; a program needn't handle non-finite values. No bound on the sum of `counts` on one device may be relied on, other than what follows from the above.
Results may differ from the reference program's by a relative error of at most 0.0073.
Values may be sent and summed in bfloat16 or wider, within the bound.
No kernel may reach another device: no remote copies, remote signals or barrier semaphores. Data moves between devices by JAX's collectives and lax.ppermute only.
A program may use at most 64 MiB of HBM per device.

```python
import math
import jax
import jax.numpy as jnp
import numpy as np
from jax import lax

SB = 2
W = 1
NS = 6144
NFFT = 8192
F = 2048
BAND = 64
LAGS = 512
CAP = 4
S = 32
SLOTS = 64
N_ROW = 16


def draw_records(key, part):
    key_noise, key_scale, key_tone, key_phase, key_amp = jax.random.split(key, 5)
    full_dims = (SLOTS, 3, W, NS)
    noise_part = jnp.clip(jax.random.normal(key_noise, full_dims, jnp.float32), -6.0, 6.0)
    amplitude = jax.random.uniform(key_amp, (SLOTS, 3, 1, 1), jnp.float32, 0.0, 2.0)
    scales = 10.0 ** jax.random.uniform(key_scale, (SLOTS, 3, W, 1), jnp.float32, 0.0, 1.0)
    tone_bin = jax.random.randint(key_tone, (SLOTS, 3, 1, 1), 1, F)
    sample = jnp.arange(NS, dtype=jnp.int32)
    phase_index = tone_bin * sample % NFFT
    start_phase = jax.random.uniform(key_phase, (SLOTS, 3, W, 1), jnp.float32, -math.pi, math.pi)
    tone_part = amplitude * jnp.sin(phase_index.astype(jnp.float32) * (2.0 * math.pi / NFFT) + start_phase)
    return ((noise_part + tone_part) * scales).astype(jnp.bfloat16)


def set_ends(entries, key, low, top_value):
    place = [jax.random.randint(jax.random.fold_in(key, axis), (), 0, length) for axis, length in enumerate(entries.shape)]
    longest = entries.shape.index(max(entries.shape))
    neighbour = place[:longest] + [(place[longest] + 1) % entries.shape[longest]] + place[longest + 1:]
    return entries.at[tuple(place)].set(low).at[tuple(neighbour)].set(top_value)


def profile(count, total, limit, slope):
    loads = [(1 << 20) // math.isqrt(rank ** slope) + 1 for rank in range(2, count + 1)]
    surplus, given = total - limit - (count - 1), [1] * (count - 1)
    while surplus > 0:
        free = [i for i in range(count - 1) if given[i] < limit]
        whole, remaining = sum([loads[i] for i in free]), surplus
        for i in free:
            addition = min(limit - given[i], max(1, remaining * loads[i] // whole), surplus)
            given[i] = given[i] + addition
            surplus = surplus - addition
    return np.array([limit] + given)


def ragged_sizes(key, amount, total, most, lean):
    if amount == 2:
        one = jax.random.randint(key, (), max(1, total - most), min(most, total - 1) + 1)
        return jnp.stack([one, total - one])
    lengths = jnp.asarray(profile(amount, total, most, lean), jnp.int32)
    couples = (amount - 1) // 2
    source_of, taker = lengths[1:1 + 2 * couples:2], lengths[2:2 + 2 * couples:2]
    slack = jnp.minimum(source_of - 1, most - taker)
    shifted = jax.random.randint(jax.random.fold_in(key, 1), (couples,), 0, 1 << 20) % (slack + 1)
    lengths = lengths.at[1:1 + 2 * couples:2].set(source_of - shifted).at[2:2 + 2 * couples:2].set(taker + shifted)
    return lengths[jax.random.permutation(jax.random.fold_in(key, 2), amount)]


def setup_inputs(seed: int = 0, part: int = 0) -> dict:
    splits = jax.random.split(jax.random.key(seed), 6)
    part_splits = jax.random.split(jax.random.fold_in(splits[5], part), 6)
    records = draw_records(jax.random.fold_in(jax.random.fold_in(splits[5], part), 71), part)
    counts = ragged_sizes(part_splits[1], N_ROW, S, CAP, 2).astype(jnp.int32)
    assign = jax.random.permutation(part_splits[2], S).astype(jnp.int32)
    station_slot = jax.random.permutation(part_splits[3], S).astype(jnp.int32)
    gap_mask = set_ends((jax.random.randint(part_splits[4], (S, W), 0, 4) < 3).astype(jnp.int32), jax.random.fold_in(part_splits[4], 1), 0, 1)
    return dict(records=records, counts=counts, assign=assign, station_slot=station_slot, gap_mask=gap_mask)


epsilon_level = 1e-06

def dft_block(first_bin, width_bins, samples, length):
    sample = jnp.arange(samples, dtype=jnp.int32)[:, None]
    bin_index = first_bin + jnp.arange(width_bins, dtype=jnp.int32)[None, :]
    phase_index = sample * bin_index % length
    angles = phase_index.astype(jnp.float32) * (2.0 * math.pi / length)
    return jnp.concatenate([jnp.cos(angles), -jnp.sin(angles)], axis=1).astype(jnp.bfloat16)

def lag_table(width_bins, lag_count, length):
    frequency = jnp.arange(width_bins, dtype=jnp.int32)[:, None]
    delays = (jnp.arange(lag_count, dtype=jnp.int32) - lag_count // 2) % length
    phase_index = frequency * delays[None, :] % length
    angles = phase_index.astype(jnp.float32) * (2.0 * math.pi / length)
    return jnp.concatenate([jnp.cos(angles), -jnp.sin(angles)], axis=0).astype(jnp.bfloat16)

def whiten(real_part, imag_part, band_width):
    amplitude = jnp.sqrt(real_part * real_part + imag_part * imag_part)
    full_shape = amplitude.shape
    banded = full_shape[:-1] + (full_shape[-1] // band_width, band_width)
    levels = lax.optimization_barrier(jnp.mean(amplitude.reshape(banded), axis=-1, keepdims=True))
    levels = jnp.broadcast_to(levels, banded).reshape(full_shape)
    return (real_part / (levels + epsilon_level), imag_part / (levels + epsilon_level))

def cross_pairs(left_rows, right_rows):
    left_real = left_rows[:, None, :, None, :, 0, :].astype(jnp.float32)
    left_imag = left_rows[:, None, :, None, :, 1, :].astype(jnp.float32)
    right_real = right_rows[None, :, None, :, :, 0, :].astype(jnp.float32)
    right_imag = right_rows[None, :, None, :, :, 1, :].astype(jnp.float32)
    real_sum = lax.optimization_barrier(jnp.sum(left_real * right_real + left_imag * right_imag, axis=4))
    imag_sum = lax.optimization_barrier(jnp.sum(left_imag * right_real - left_real * right_imag, axis=4))
    return jnp.stack([real_sum, imag_sum], axis=4).astype(jnp.bfloat16)

def project(cross_block, lag_rows):
    row_total = cross_block.shape[0]
    flat_cross = cross_block.reshape(-1, lag_rows.shape[0])
    product = jnp.dot(flat_cross, lag_rows, preferred_element_type=jnp.float32)
    return product.reshape(row_total, -1, 9, lag_rows.shape[1])

def reference(records, counts, assign, station_slot, gap_mask):
    positions = jnp.arange(S, dtype=jnp.int32)
    row_station = jnp.zeros((S,), jnp.int32).at[station_slot].set(positions)
    station_place = jnp.zeros((S,), jnp.int32).at[assign].set(positions)
    reader_ends = jnp.cumsum(counts).astype(jnp.int32)
    reader_starts = (reader_ends - counts).astype(jnp.int32)
    place_of_row = station_place[row_station]
    reader_of_row = lax.optimization_barrier(jnp.sum((reader_ends[None, :] <= place_of_row[:, None]).astype(jnp.int32), axis=1)).astype(jnp.int32)
    slot_of_row = (reader_of_row * CAP + place_of_row - reader_starts[reader_of_row]).astype(jnp.int32)
    row_records = records[slot_of_row]
    row_present = gap_mask[row_station]
    table_full = dft_block(jnp.int32(0), F, NS, NFFT)
    spectrum = jnp.dot(row_records.reshape(S * 3 * W, NS), table_full, preferred_element_type=jnp.float32)
    white_real, white_imag = whiten(spectrum[:, :F], spectrum[:, F:], BAND)
    present_rows = jnp.broadcast_to(row_present[:, None, :], (S, 3, W)).reshape(S * 3 * W, 1).astype(jnp.float32)
    spectra = jnp.stack([white_real * present_rows, white_imag * present_rows], axis=1).astype(jnp.bfloat16)
    spectra = spectra.reshape(S, 3, W, 2, F)
    lag_rows = lag_table(F, LAGS, NFFT)
    present_float = row_present.astype(jnp.float32)

    def row_block(block_index):
        left_rows = lax.dynamic_slice_in_dim(spectra, block_index * SB, SB, 0)
        left_present = lax.dynamic_slice_in_dim(present_float, block_index * SB, SB, 0)
        raw_lags = project(cross_pairs(left_rows, spectra), lag_rows)
        common = jnp.dot(left_present, present_float.T, precision=lax.Precision.HIGHEST)
        return raw_lags / (jnp.maximum(common, 1.0)[:, :, None, None] * math.sqrt(F))
    blocks = lax.map(row_block, jnp.arange(N_ROW, dtype=jnp.int32))
    return blocks.reshape(S, S, 9, LAGS)
```

```python
import functools
import math

import jax
import jax.numpy as jnp
from jax import lax
from jax.experimental import pallas as pl
from jax.experimental.pallas import tpu as pltpu
from jax.sharding import PartitionSpec as P

NFFT = 8192
F = 2048
BAND = 64
LAGS = 512
EPS = 1e-06

K1 = 64
K2 = F // K1
N2 = NFFT // K1
LANES = 128
META = 16
COLS = 32
F32 = jnp.float32
BF16 = jnp.bfloat16


def iota(shape, dim):
    return lax.broadcasted_iota(jnp.int32, shape, dim)


def cos_sin(phase):
    phase = phase & (NFFT - 1)
    shifted = phase + NFFT // 8
    quadrant = (shifted >> 11) & 3
    angle = ((shifted & 2047) - NFFT // 8).astype(F32) * F32(2.0 * math.pi / NFFT)
    square = angle * angle
    sine = angle * (
        1.0 + square * (-1 / 6 + square * (1 / 120 + square * (-1 / 5040 + square * (1 / 362880))))
    )
    cosine = 1.0 + square * (
        -0.5 + square * (1 / 24 + square * (-1 / 720 + square * (1 / 40320 - square * (1 / 3628800))))
    )
    swap = (quadrant & 1) == 1
    c = jnp.where(swap, sine, cosine)
    s = jnp.where(swap, cosine, sine)
    c = jnp.where((quadrant == 1) | (quadrant == 2), -c, c)
    s = jnp.where(quadrant >= 2, -s, s)
    return c, s


def halves(value):
    high = value.astype(BF16)
    return high, (value - high.astype(F32)).astype(BF16)


def matmul(left, right):
    return jnp.dot(left, right, preferred_element_type=F32)


def matmul_nt(left, right):
    return lax.dot_general(left, right, (((1,), (1,)), ((), ())), preferred_element_type=F32)


def spectra_kernel(slots, counts_ref, x_ref, out_ref):
    channels, depth, _ = x_ref.shape
    k1 = iota((K1, depth), 0)
    column = iota((K1, depth), 1)
    c1, s1 = cos_sin(k1 * (column // slots) * (NFFT // K1))
    owner = column % slots
    rows = [jnp.where(owner == s, t, 0.0) for t in (c1, -s1) for s in range(slots)]
    first = jnp.concatenate(rows, axis=0)
    first = jnp.concatenate(halves(first), axis=1)
    ct, st = cos_sin(iota((K1, N2), 0) * iota((K1, N2), 1))
    ct = jnp.concatenate([ct] * slots, axis=0)
    st = jnp.concatenate([st] * slots, axis=0)
    c2, s2 = cos_sin(iota((K2, N2), 0) * iota((K2, N2), 1) * (NFFT // N2))
    second = jnp.concatenate(
        [jnp.concatenate([c2, s2], axis=1), jnp.concatenate([-s2, c2], axis=1)], axis=0
    )
    second_high, second_low = halves(second)
    second_both = jnp.concatenate([second_high, second_low], axis=0)
    ones = jnp.where(iota((LANES, LANES), 0) // BAND == iota((LANES, LANES), 1) // BAND, 1.0 / BAND, 0.0)
    ones = jnp.concatenate([ones, ones], axis=0).astype(BF16)
    low_lanes = iota((K2, LANES), 1) < K1
    half = slots * K1
    for c in range(channels):
        x = x_ref[c]
        y = matmul(first, jnp.concatenate([x, x], axis=0))
        y_re, y_im = y[:half], y[half:]
        b = jnp.concatenate([y_re * ct + y_im * st, y_im * ct - y_re * st], axis=1)
        b_high, b_low = halves(b)
        z = matmul_nt(second_both, b_high)
        z = z[: 2 * K2] + z[2 * K2 :] + matmul_nt(second_high, b_low)
        for pair in range(slots // 2):
            lanes = slice(pair * LANES, (pair + 1) * LANES)
            re, im = z[:K2, lanes], z[K2:, lanes]
            amplitude = jnp.sqrt(re * re + im * im)
            level = matmul(jnp.concatenate(halves(amplitude), axis=1), ones)
            scale = 1.0 / (level + EPS)
            re, im = re * scale, im * scale
            even = jnp.where(low_lanes, re, pltpu.roll(im, K1, 1))
            odd = jnp.where(low_lanes, pltpu.roll(re, K1, 1), im)
            for s, tile in ((2 * pair, even), (2 * pair + 1, odd)):
                at = (s * channels + c) * K2
                out_ref[at : at + K2, :] = tile.astype(BF16)
    end = slots * channels * K2
    out_ref[end : end + META, :] = jnp.full((META, LANES), counts_ref[0].astype(F32)).astype(BF16)


def lag_kernel(after_ref, out_ref, c2_ref, s2_ref):
    j = iota((K1, LAGS), 1)
    t = (j - LAGS // 2) & (NFFT - 1)
    c1, s1 = cos_sin(iota((K1, LAGS), 0) * t)
    j2 = iota((K2, LAGS), 1)
    t2 = (j2 - LAGS // 2) & (NFFT - 1)
    c2_ref[...], s2_ref[...] = cos_sin(iota((K2, LAGS), 0) * t2 * K1)

    def block(k2, carry):
        c2 = c2_ref[pl.ds(k2, 1), :]
        s2 = s2_ref[pl.ds(k2, 1), :]
        both = jnp.concatenate([c1 * c2 - s1 * s2, -(s1 * c2 + c1 * s2)], axis=0)
        out_ref[pl.ds(pl.multiple_of(k2 * 2 * K1, 2 * K1), 2 * K1), :] = both.astype(BF16)
        return carry

    lax.fori_loop(0, K2, block, 0)


def correlate_kernel(
    masks, slots, channels, own, stations, chunk,
    place_ref, assign_ref, row_ref, gap_ref, lag_ref, *refs
):
    blocks = refs[: len(masks) if masks else 1]
    out_ref, b_ref, a_ref, present_ref, left_ref, acc_ref = refs[len(blocks) :]
    groups = stations // COLS
    stride = channels * COLS
    size = slots * channels * K2 + META
    meta = slots * channels * K2
    lane = iota((8, LANES), 1)
    me = place_ref[0]

    def counted(ref, base, source):
        tile = ref[pl.ds(pl.multiple_of(base + meta, META), META), :].astype(F32)
        return jnp.where(lane == source, tile[:8], 0.0)

    if masks:
        sources = [me ^ mask for mask in masks]
        table = functools.reduce(
            jnp.add, [counted(ref, 0, source) for ref, source in zip(blocks, sources)]
        )
    else:
        total = blocks[0].shape[0] // size
        table = lax.fori_loop(
            0, total, lambda o, v: v + counted(blocks[0], o * size, o), jnp.zeros((8, LANES), F32)
        )

    def spread(ref, base, source):
        offset = (jnp.sum(jnp.where(lane < source, table, 0.0)) / 8.0).astype(jnp.int32)
        count = (jnp.sum(jnp.where(lane == source, table, 0.0)) / 8.0).astype(jnp.int32)
        for s in range(slots):
            @pl.when(s < count)
            def _():
                station = assign_ref[jnp.minimum(offset + s, stations - 1)]
                row = row_ref[station]
                mask = gap_ref[station].astype(F32)
                group, column = row // COLS, row % COLS
                present_ref[pl.ds(row, 1), :] = jnp.full((1, LANES), mask)
                for c in range(channels):
                    at = base + (s * channels + c) * K2
                    tile = ref[pl.ds(pl.multiple_of(at, 16), K2), :].astype(F32) * mask
                    start = group * (K2 * stride) + c * COLS + column
                    b_ref[pl.ds(start, K2, stride=stride), :] = tile

    if masks:
        for ref, source in zip(blocks, sources):
            spread(ref, 0, source)
    else:
        lax.fori_loop(0, total, lambda o, v: (spread(blocks[0], o * size, o), v)[1], 0)

    low = iota((K2, LANES), 1) < K1
    for a in range(own):
        row = me * own + a
        group, column = row // COLS, row % COLS
        for c in range(channels):
            start = group * (K2 * stride) + c * COLS + column
            tile = b_ref[pl.ds(start, K2, stride=stride), :]
            q = a * channels + c
            swapped = pltpu.roll(tile, K1, 1)
            a_ref[q, :K2, :] = jnp.where(low, tile, -swapped)
            a_ref[q, K2:, :] = jnp.where(low, swapped, tile)

    rows = own * channels
    width = chunk * LANES

    def column_group(group, carry):
        for step in range(K2 // chunk):
            for kk in range(chunk):
                k2 = step * chunk + kk
                base = pl.multiple_of(group * (K2 * stride) + k2 * stride, 8)
                b = b_ref[pl.ds(base, stride), :]
                b_swapped = pltpu.roll(b, K1, 1)
                for q in range(rows):
                    cross = a_ref[q, k2 : k2 + 1, :] * b + a_ref[q, K2 + k2 : K2 + k2 + 1, :] * b_swapped
                    left_ref[step % 2, q * stride : (q + 1) * stride, kk * LANES : (kk + 1) * LANES] = (
                        cross.astype(BF16)
                    )
            product = matmul(left_ref[step % 2], lag_ref[step * width : (step + 1) * width, :])
            if step == 0:
                acc_ref[...] = product
            else:
                acc_ref[...] += product
        for a in range(own):
            first = pl.multiple_of(group * COLS, 8)
            common = present_ref[pl.ds(first, COLS), :] * present_ref[pl.ds(me * own + a, 1), :]
            scale = 1.0 / (jnp.maximum(common, 1.0) * math.sqrt(F))
            scale = jnp.concatenate([scale] * (LAGS // LANES), axis=1)
            for c in range(channels):
                for d in range(channels):
                    at = (a * channels + c) * stride + d * COLS
                    out_ref[a, channels * c + d, pl.ds(first, COLS), :] = acc_ref[at : at + COLS, :] * scale
        return carry

    if groups == 1:
        column_group(0, 0)
    else:
        lax.fori_loop(0, groups, column_group, 0)


def swap_with(bits, total):
    return [(i, i ^ bits) for i in range(total)]


def gather_blocks(block, total):
    if total != 16:
        return [lax.all_gather(block, "row", axis=0, tiled=True)], None

    def send(value, bits):
        return lax.ppermute(value, "row", swap_with(bits, total))

    far = send(block, 8)
    near = [(block, 0), (far, 8)]
    for bits in (4, 2, 6):
        near.append((send(block, bits), bits))
    for bits in (4, 2, 6):
        near.append((send(far, bits), 8 ^ bits))
    near += [(send(value, 1), bits ^ 1) for value, bits in near]
    return [value for value, _ in near], tuple(bits for _, bits in near)


def whole_spec(space):
    return pl.BlockSpec(memory_space=space)


def on_device(records, counts, assign, station_slot, gap_mask):
    slots, channels, windows, samples = records.shape
    stations = assign.shape[0]
    total = lax.axis_size("row")
    own = stations // total
    assert windows == 1 and slots % 2 == 0 and samples % LANES == 0 and stations % COLS == 0
    depth = samples // LANES
    x = jnp.transpose(records.reshape(slots, channels, depth, LANES), (1, 2, 0, 3))
    x = x.reshape(channels, depth * slots, LANES)
    size = slots * channels * K2 + META
    block = pl.pallas_call(
        functools.partial(spectra_kernel, slots),
        out_shape=jax.ShapeDtypeStruct((size, LANES), BF16),
        in_specs=[whole_spec(pltpu.SMEM), whole_spec(pltpu.VMEM)],
        out_specs=whole_spec(pltpu.VMEM),
        compiler_params=pltpu.CompilerParams(vmem_limit_bytes=16 << 20),
        cost_estimate=pl.CostEstimate(flops=1 << 29, bytes_accessed=1 << 19, transcendentals=0),
        name="spectra",
    )(counts, x)
    lag_rows = pl.pallas_call(
        lag_kernel,
        out_shape=jax.ShapeDtypeStruct((2 * F, LAGS), BF16),
        in_specs=[whole_spec(pl.ANY)],
        out_specs=whole_spec(pltpu.VMEM),
        scratch_shapes=[pltpu.VMEM((K2, LAGS), F32), pltpu.VMEM((K2, LAGS), F32)],
        compiler_params=pltpu.CompilerParams(vmem_limit_bytes=16 << 20),
        cost_estimate=pl.CostEstimate(flops=1 << 24, bytes_accessed=1 << 22, transcendentals=0),
        name="lag_rows",
    )(block)
    blocks, masks = gather_blocks(block, total)
    place = lax.axis_index("row").astype(jnp.int32).reshape(1)
    chunk = 8
    rows = own * channels
    stride = channels * COLS
    product = pl.pallas_call(
        functools.partial(correlate_kernel, masks, slots, channels, own, stations, chunk),
        out_shape=jax.ShapeDtypeStruct((own, channels * channels, stations, LAGS), F32),
        in_specs=[whole_spec(pltpu.SMEM)] * 4 + [whole_spec(pltpu.VMEM)] * (1 + len(blocks)),
        out_specs=whole_spec(pltpu.VMEM),
        scratch_shapes=[
            pltpu.VMEM((stations // COLS * K2 * stride, LANES), F32),
            pltpu.VMEM((rows, 2 * K2, LANES), F32),
            pltpu.VMEM((stations, LANES), F32),
            pltpu.VMEM((2, rows * stride, chunk * LANES), BF16),
            pltpu.VMEM((rows * stride, LAGS), F32),
        ],
        compiler_params=pltpu.CompilerParams(vmem_limit_bytes=40 << 20),
        cost_estimate=pl.CostEstimate(flops=1 << 31, bytes_accessed=8 << 20, transcendentals=0),
        name="correlate",
    )(place, assign, station_slot, gap_mask.reshape(stations), lag_rows, *blocks)
    return jnp.swapaxes(product, 1, 2)


def solution(mesh):
    return jax.shard_map(
        on_device,
        mesh=mesh,
        in_specs=(
            P(("parts", "row"), None, None, None),
            P(("parts", "row")),
            P("parts"),
            P("parts"),
            P("parts", None),
        ),
        out_specs=P(("parts", "row"), None, None, None),
        check_vma=False,
    )
```
